128 devices in a mesh: ctx: 8 (over x, z_lo), head: 16 (over z_hi, y, core).
Axes of the slice: x: 4, y: 4, z: 4 (z_hi: 2, z_lo: 2; z = z_hi * 2 + z_lo), core: 2. Of those that a mesh axis runs over, the one named last changes fastest.
Arguments:
- queries: bfloat16 [256, 16384], P(None, 'head'), may hold values from -64 to 64, as said below
- grad_out: bfloat16 [256, 16384], P(None, 'head'), may hold values from -24 to 24
- latent: bfloat16 [16384, 512], P(('ctx', 'head')), may hold values from -6.1 to 6.1
- up_key: bfloat16 [512, 16384], P(None, 'head'), as said below
- up_value: bfloat16 [512, 16384], P(None, 'head'), may hold values from -0.25 to 0.25
Outputs:
- grad_queries: float32 [256, 16384], P('ctx', 'head')
- grad_latent: float32 [16384, 512], P(('ctx', 'head'))
- grad_up_key: float32 [512, 16384], P('ctx', 'head')
- grad_up_value: float32 [512, 16384], P('ctx', 'head')
The draws below stay inside these ranges and needn't reach their ends.
Inputs may be any that keep to these rules, and one draw needn't show every extreme that they name: `queries`: entries lie within 64 in magnitude. `up_key`: entries lie within 4 / sqrt(512) in magnitude.
All inputs are finite; a program needn't handle non-finite values.
Results may differ from the reference program's by a relative error of at most 0.005.
Values may be sent and summed in bfloat16 or wider, within the bound.
A program may use at most 128 MiB of HBM per device.

```python
import math
import jax
import jax.numpy as jnp
from jax import lax

HEADS = 128
HD = 128
LATENT = 512
QTOK = 256
CTX_LEN = 16384


def shared_arrays(key):
    base = jax.random.fold_in(key, 7001)
    normal = jnp.clip(jax.random.normal(jax.random.fold_in(base, 1), (CTX_LEN, LATENT), jnp.float32), -4.0, 4.0)
    rising = 0.6 + 0.7 * jnp.arange(CTX_LEN, dtype=jnp.float32) / CTX_LEN
    jitter = jnp.exp(jax.random.uniform(jax.random.fold_in(base, 2), (CTX_LEN, 1), jnp.float32, -0.15, 0.15))
    latent = normal * rising[:, None] * jitter
    up_key = jnp.clip(jax.random.normal(jax.random.fold_in(base, 3), (LATENT, HEADS * HD), jnp.float32), -4.0, 4.0) / math.sqrt(LATENT)
    return (latent, up_key)


def draw_latent(key, part):
    return shared_arrays(key)[0].astype(jnp.bfloat16)


def draw_up_key(key, part):
    return shared_arrays(key)[1].astype(jnp.bfloat16)


def draw_queries(key, part):
    drawn = jnp.clip(jax.random.normal(jax.random.fold_in(key, 41), (QTOK, HEADS * HD), jnp.float32), -4.0, 4.0)
    return jnp.clip(drawn, -64.0, 64.0).astype(jnp.bfloat16)


def shard_levels(stream_key, extent, cuts, low, top_value):
    gain, own = 1.0, jax.random.fold_in(stream_key, 6)
    for dim, parts in cuts:
        steps = jnp.exp(jax.random.uniform(jax.random.fold_in(own, dim), (parts,), jnp.float32, low / len(cuts), top_value / len(cuts)))
        gain = gain * jnp.repeat(steps, extent[dim] // parts).reshape([-1 if axis == dim else 1 for axis in range(len(extent))])
    return gain


def normal_values(own_key, extent, width, bound, split=(), kind=jnp.bfloat16):
    result = jax.random.normal(own_key, extent, jnp.float32) * width
    if len(split) > 0:
        result = shard_levels(own_key, extent, split, -0.22, 0.18) * result
    return jnp.clip(result, min=-bound, max=bound).astype(kind)


def setup_inputs(seed: int = 0) -> dict:
    arg_keys = jax.random.split(jax.random.key(seed), 6)
    return {
        "queries": draw_queries(jax.random.fold_in(arg_keys[5], 71), 0),
        "grad_out": normal_values(arg_keys[1], (QTOK, HEADS * HD), 4.0, 24.0, ((1, 16),)),
        "latent": draw_latent(jax.random.fold_in(arg_keys[5], 71), 0),
        "up_key": draw_up_key(jax.random.fold_in(arg_keys[5], 71), 0),
        "up_value": normal_values(arg_keys[4], (LATENT, HEADS * HD), LATENT ** -0.5, 0.25, ((1, 16),)),
    }


def reference(queries, grad_out, latent, up_key, up_value):
    scale = 1.0 / math.sqrt(HD)
    query_pos = CTX_LEN - QTOK + jnp.arange(QTOK, dtype=jnp.int32)
    key_pos = jnp.arange(CTX_LEN, dtype=jnp.int32)
    visible = key_pos[None, :] <= query_pos[:, None]

    def one_head(carry, head_index):
        offset = head_index * HD
        query_head = lax.dynamic_slice_in_dim(queries, offset, HD, 1)
        grad_head = lax.dynamic_slice_in_dim(grad_out, offset, HD, 1)
        key_weight = lax.dynamic_slice_in_dim(up_key, offset, HD, 1)
        value_weight = lax.dynamic_slice_in_dim(up_value, offset, HD, 1)
        key_head = jnp.dot(latent, key_weight, preferred_element_type=jnp.float32)
        value_head = jnp.dot(latent, value_weight, preferred_element_type=jnp.float32).astype(jnp.bfloat16)
        raw = jnp.dot(query_head.astype(jnp.float32), key_head.T, precision=lax.Precision.HIGHEST) * scale
        scores = jnp.where(visible, raw, -jnp.inf)
        maxima = lax.optimization_barrier(jnp.max(scores, axis=1))
        weights = jnp.exp(scores - maxima[:, None])
        totals = lax.optimization_barrier(jnp.sum(weights, axis=1))
        probs = weights / totals[:, None]
        grad_probs = jnp.dot(grad_head, value_head.T, preferred_element_type=jnp.float32)
        deltas = lax.optimization_barrier(jnp.sum(probs * grad_probs, axis=1))
        grad_scores = (probs * (grad_probs - deltas[:, None]) * scale).astype(jnp.bfloat16)
        query_grad = jnp.dot(grad_scores.astype(jnp.float32), key_head, precision=lax.Precision.HIGHEST)
        key_grad = jnp.dot(grad_scores.T, query_head, preferred_element_type=jnp.float32).astype(jnp.bfloat16)
        value_grad = jnp.dot(probs.astype(jnp.bfloat16).T, grad_head, preferred_element_type=jnp.float32).astype(jnp.bfloat16)
        latent_part = jnp.dot(key_grad, key_weight.T, preferred_element_type=jnp.float32) + jnp.dot(value_grad, value_weight.T, preferred_element_type=jnp.float32)
        key_weight_grad = jnp.dot(latent.T, key_grad, preferred_element_type=jnp.float32)
        value_weight_grad = jnp.dot(latent.T, value_grad, preferred_element_type=jnp.float32)
        return (carry + latent_part, (query_grad, key_weight_grad, value_weight_grad))
    initial = jnp.zeros((CTX_LEN, LATENT), jnp.float32)
    grad_latent, stacked = lax.scan(one_head, initial, jnp.arange(HEADS, dtype=jnp.int32))
    grad_queries = jnp.transpose(stacked[0], (1, 0, 2)).reshape(QTOK, HEADS * HD)
    grad_up_key = jnp.transpose(stacked[1], (1, 0, 2)).reshape(LATENT, HEADS * HD)
    grad_up_value = jnp.transpose(stacked[2], (1, 0, 2)).reshape(LATENT, HEADS * HD)
    return (grad_queries, grad_latent, grad_up_key, grad_up_value)
```

```python
import math

import jax
import jax.numpy as jnp
from jax import lax
from jax.experimental import pallas as pl
from jax.experimental.pallas import tpu as pltpu
from jax.sharding import PartitionSpec as P

HD = 128
NH = 8
ROWS = 2048
TILE = 256
NQ = 256
NEG = -1e30
F32 = jnp.float32
BF16 = jnp.bfloat16
MESH = pl.DeviceIdType.MESH
SCALE = 1.0 / math.sqrt(HD)
TN = (((0,), (0,)), ((), ()))


def dot(a, b):
    return jnp.dot(a, b, preferred_element_type=F32)


def kernel(
    q_ref, go_ref, own_ref, upk_ref, upv_ref,
    gq_out, gl_out, gk_out, gv_out,
    lat, lat_t, up_t, q_t, go_t, kk, ebuf, gbuf, bias,
    mst, tst, dst, st_all, wst, delta, acc,
    pbuf, r1, rd, r2, rz, zs, fsum,
    gds, gdr, ys, yr, lzs, lzr,
    ag_send, ag_recv, st_send, st_recv,
    s1_send, s1_recv, sd_send, sd_recv, s2_send, s2_recv, sz_send, sz_recv,
    gd_send, gd_recv, y_send, y_recv, lz_send, lz_recv,
):
    ci = lax.axis_index("ctx")
    hi = lax.axis_index("head")
    x, zl = ci // 2, ci % 2
    zh, y, core = hi // 8, (hi // 2) % 4, hi % 2
    oz = 1 - zh

    def ym(d):
        return (y + d) % 4

    def xm(d):
        return (x + d) % 4

    partner = (ci, zh * 8 + y * 2 + 1 - core)
    ydev = {s: (ci, zh * 8 + ym(s) * 2 + core) for s in (1, 3)}
    zdev = (x * 2 + 1 - zl, oz * 8 + y * 2 + core)
    xdev = {s: (xm(s) * 2 + zl, hi) for s in (1, 3)}
    rdev = (x * 2 + 1 - zl, hi)
    peers = [((ci + d) % 8, hi) for d in range(1, 8)]

    barrier = pltpu.get_barrier_semaphore()
    for d in [partner, ydev[1], ydev[3], zdev] + peers:
        pl.semaphore_signal(barrier, inc=1, device_id=d, device_id_type=MESH)

    def remote(src, dst, ss, rs, device):
        return pltpu.make_async_remote_copy(
            src_ref=src, dst_ref=dst, send_sem=ss, recv_sem=rs,
            device_id=device, device_id_type=MESH,
        )

    def slot(z_, y_, c_):
        return z_ * 8 + y_ * 2 + c_

    def ag(index, s, device, src=None):
        rows = lat.at[pl.ds(pl.multiple_of(s * 128, 128), 128), :]
        return remote(rows if src is None else src, rows, ag_send.at[index], ag_recv.at[s], device)

    s_o, s_z = slot(zh, y, core), slot(oz, y, core)
    s_l, s_lz = slot(zh, ym(3), core), slot(oz, ym(3), core)
    s_r, s_rz = slot(zh, ym(1), core), slot(oz, ym(1), core)
    s_f, s_fz = slot(zh, ym(2), core), slot(oz, ym(2), core)
    arrivals = {
        0: (s_o, ((0, zdev), (1, ydev[1]), (2, ydev[3]), (3, partner))),
        1: (s_z, ((4, ydev[1]), (5, ydev[3]), (6, partner))),
        2: (s_l, ((7, ydev[1]), (8, partner))),
        3: (s_lz, ((10, partner),)),
        4: (s_r, ((9, partner),)),
        5: (s_rz, ((11, ydev[3]), (12, partner))),
        6: (s_f, ((13, partner),)),
        7: (s_fz, ((14, partner),)),
    }
    other = {
        k: s + 1 - 2 * core for k, (s, _) in arrivals.items()
    }

    def arrive(k):
        s, sends = arrivals[k]
        ag(sends[0][0], s, partner).wait_recv()
        for index, device in sends:
            ag(index, s, device).start()

    lat[pl.ds(pl.multiple_of(s_o * 128, 128), 128), :] = own_ref[...]
    pl.semaphore_wait(barrier, 11)
    for index, device in arrivals[0][1]:
        ag(index, s_o, device, own_ref).start()

    for h in range(NH):
        cols = slice(h * HD, (h + 1) * HD)
        q_t[h] = q_ref[:, cols].T
        go_t[h] = go_ref[:, cols].T

    @pl.loop(0, NH)
    def _(h):
        cols = pl.ds(pl.multiple_of(h * HD, HD), HD)
        rows = pl.multiple_of(h * 2 * HD, 2 * HD)
        up_t[pl.ds(rows, HD), :] = upk_ref[:, cols].T
        up_t[pl.ds(rows + HD, HD), :] = upv_ref[:, cols].T

    last_owner = jnp.logical_and(x == 3, zl == zh)
    key_row = lax.broadcasted_iota(jnp.int32, (TILE, NQ), 0)
    query_col = lax.broadcasted_iota(jnp.int32, (TILE, NQ), 1)

    @pl.loop(0, 8)
    def _(step):
        for k in range(1, 8):
            @pl.when(step == max(k - 1, 1))
            def _(k=k):
                arrive(k)
        for k in range(8):
            @pl.when(step == k)
            def _(k=k):
                ag(arrivals[k][1][0][0], other[k], partner).wait_recv()
        v = (3 * (step // 2)) % 5
        y_t = (y + v - 2 * (v // 4)) % 4
        z_t = (zh + step % 2) % 2
        t = z_t * 4 + y_t
        rows = pl.ds(pl.multiple_of(t * TILE, TILE), TILE)
        limit = jnp.where(jnp.logical_and(last_owner, t == 7), 0, 4 * TILE)
        bias[...] = jnp.where(key_row > query_col + limit, NEG, 0.0)
        block = lat[rows, :]
        lat_t[:, rows] = block.T
        for pair in range(NH // 2):
            cols = slice(pair * 2 * HD, (pair + 1) * 2 * HD)
            k2 = dot(block, upk_ref[:, cols])
            v2 = dot(block, upv_ref[:, cols]).astype(BF16)
            for b in range(2):
                h = pair * 2 + b
                half = slice(b * HD, (b + 1) * HD)
                key = k2[:, half]
                key_hi = key.astype(BF16)
                key_lo = (key - key_hi.astype(F32)).astype(BF16)
                both = jnp.concatenate([key_hi, key_lo], axis=1)
                kk[rows, h * 256:(h + 1) * 256] = both
                qt = q_t[h]
                s = dot(both, jnp.concatenate([qt, qt], axis=0)) + bias[...]
                g = dot(v2[:, half], go_t[h])
                m = jnp.max(s, axis=0, keepdims=True)
                e = jnp.exp((s - m) * SCALE)
                ebuf[h, rows, :] = e
                gbuf[h, rows, :] = g
                mst[h, pl.ds(t, 1), :] = m
                tst[h, pl.ds(t, 1), :] = jnp.sum(e, axis=0, keepdims=True)
                dst[h, pl.ds(t, 1), :] = jnp.sum(e * g, axis=0, keepdims=True)

    for h in range(NH):
        mt = mst[h]
        m = jnp.max(mt, axis=0, keepdims=True)
        w = jnp.exp((mt - m) * SCALE)
        st_all[ci, h:h + 1, :] = m
        st_all[ci, NH + h:NH + h + 1, :] = jnp.sum(w * tst[h], axis=0, keepdims=True)
        st_all[ci, 2 * NH + h:2 * NH + h + 1, :] = jnp.sum(w * dst[h], axis=0, keepdims=True)

    def stat(d, index):
        return remote(st_all.at[index], st_all.at[index], st_send.at[d - 1], st_recv.at[index], peers[d - 1])

    for d in range(1, 8):
        stat(d, ci).start()
    for d in range(1, 8):
        stat(d, (ci + d) % 8).wait_recv()
    m_all = st_all[0, 0:NH, :]
    for c in range(1, 8):
        m_all = jnp.maximum(m_all, st_all[c, 0:NH, :])
    total = jnp.zeros((NH, NQ), F32)
    product = jnp.zeros((NH, NQ), F32)
    for c in range(8):
        w = jnp.exp((st_all[c, 0:NH, :] - m_all) * SCALE)
        total += w * st_all[c, NH:2 * NH, :]
        product += w * st_all[c, 2 * NH:3 * NH, :]
    delta[...] = product / total
    inverse = 1.0 / total
    for h in range(NH):
        wst[h] = jnp.exp((mst[h] - m_all[h:h + 1]) * SCALE) * inverse[h:h + 1]

    def stage1(h, s):
        return remote(pbuf.at[h, xm(2)], r1.at[h], s1_send.at[h], s1_recv.at[h], xdev[s])

    def direct(h, s):
        return remote(pbuf.at[h, xm(-s)], rd.at[h], sd_send.at[h], sd_recv.at[h], xdev[4 - s])

    def stage2(h, s):
        return remote(pbuf.at[h, xm(s)], r2.at[h], s2_send.at[h], s2_recv.at[h], xdev[s])

    def stagez(h):
        return remote(zs.at[h], rz.at[h], sz_send.at[h], sz_recv.at[h], rdev)

    def up_relay(h, s):
        stage1(h, s).wait_recv()
        pbuf[h, xm(s)] = (pbuf[h, xm(s)].astype(F32) + r1[h].astype(F32)).astype(BF16)
        stage2(h, s).start()

    def up_join(h, s):
        direct(h, s).wait_recv()
        stage2(h, s).wait_recv()

        def part(z_):
            return pbuf[h, x, z_].astype(F32) + rd[h, z_].astype(F32) + r2[h, z_].astype(F32)

        zs[h] = part(1 - zl).astype(BF16)
        stagez(h).start()
        fsum[h] = part(zl)

    @pl.loop(0, NH // 2)
    def _(hp):
        qcols = pl.ds(pl.multiple_of(hp * 2 * HD, 2 * HD), 2 * HD)
        q2 = q_ref[:, qcols]
        go2 = go_ref[:, qcols]
        acc[...] = jnp.zeros_like(acc)

        @pl.loop(0, 8)
        def _(t):
            rows = pl.ds(pl.multiple_of(t * TILE, TILE), TILE)
            for b in range(2):
                h = hp * 2 + b
                kcols = pl.ds(pl.multiple_of(h * 256, 256), 256)
                e = ebuf[h, rows, :]
                w = wst[h, pl.ds(t, 1), :]
                prob = e * w
                gs = (prob * (gbuf[h, rows, :] - delta[pl.ds(h, 1), :]) * SCALE).astype(BF16)
                acc[b] += lax.dot_general(gs, kk[rows, kcols], TN, preferred_element_type=F32)
                half = slice(b * HD, (b + 1) * HD)
                gk = dot(gs, q2[:, half]).astype(BF16)
                gv = dot(prob.astype(BF16), go2[:, half]).astype(BF16)
                kk[rows, kcols] = jnp.concatenate([gk, gv], axis=1)

        for b in range(2):
            h = hp * 2 + b
            s = 1 if b == 0 else 3
            kcols = pl.ds(pl.multiple_of(h * 256, 256), 256)
            gq = acc[b, :, 0:HD] + acc[b, :, HD:2 * HD]
            up = dot(lat_t[...], kk[:, kcols]).astype(BF16)
            for x_ in range(4):
                for z_ in range(2):
                    first = x_ * 128 + z_ * 64
                    pbuf[h, x_, z_, 0:64, :] = up[first:first + 64, :]
                    first = x_ * 64 + z_ * 32
                    pbuf[h, x_, z_, 64:80, :] = jnp.concatenate(
                        [gq[first:first + 16], gq[first + 16:first + 32]], axis=1
                    ).astype(BF16)
            stage1(h, s).start()
            direct(h, s).start()

        @pl.when(hp >= 1)
        def _():
            up_relay(hp * 2 - 2, 1)
            up_relay(hp * 2 - 1, 3)

        @pl.when(hp >= 2)
        def _():
            up_join(hp * 2 - 4, 1)
            up_join(hp * 2 - 3, 3)

    def pairwise(d):
        return remote(gds.at[d], gdr.at[d], gd_send.at[d], gd_recv.at[d], partner)

    def latent_part(d):
        y_ = ym(d)
        for z_ in range(2):
            first = pl.multiple_of((z_ * 4 + y_) * TILE, TILE)
            part = dot(kk[pl.ds(first, TILE), :], up_t[...])
            acc[0] = part[:, 0:256]
            acc[1] = part[:, 256:512]
            mine = pl.ds(pl.multiple_of(core * 128, 128), 128)
            theirs = pl.ds(pl.multiple_of((1 - core) * 128, 128), 128)
            for b in range(2):
                ebuf[b, pl.ds(d * 256 + z_ * 128, 128), :] = acc[b, mine, :]
                gds[d, b, z_] = acc[b, theirs, :].astype(BF16)
        pairwise(d).start()

    def held(d, b):
        pieces = []
        for z_ in range(2):
            pieces.append(ebuf[b, pl.ds(d * 256 + z_ * 128, 128), :] + gdr[d, b, z_].astype(F32))
        return pieces

    def ycopy(b, kind, s):
        return remote(ys.at[b, kind], yr.at[b, kind], y_send.at[b, kind], y_recv.at[b, kind], ydev[s])

    def ysend(b, kind, s, pieces):
        for z_ in range(2):
            ys[b, kind, z_] = pieces[z_].astype(BF16)
        ycopy(b, kind, s).start()

    DIRS = ((0, 1), (1, 3))
    latent_part(2)
    up_relay(6, 1)
    up_relay(7, 3)
    latent_part(1)
    pairwise(2).wait_recv()
    for b, s in DIRS:
        ysend(b, 0, s, held(2, b))
    latent_part(3)
    up_join(4, 1)
    up_join(5, 3)
    pairwise(1).wait_recv()
    pairwise(3).wait_recv()
    for b, s in DIRS:
        ysend(b, 1, 4 - s, held(4 - s, b))
    latent_part(0)
    for b, s in DIRS:
        ycopy(b, 0, s).wait_recv()
        pieces = held(s, b)
        ysend(b, 2, s, [pieces[z_] + yr[b, 0, z_].astype(F32) for z_ in range(2)])
    up_join(6, 1)
    up_join(7, 3)
    pairwise(0).wait_recv()
    for b, s in DIRS:
        ycopy(b, 1, 4 - s).wait_recv()
        ycopy(b, 2, s).wait_recv()
        pieces = held(0, b)
        for z_ in range(2):
            total_piece = pieces[z_] + yr[b, 1, z_].astype(F32) + yr[b, 2, z_].astype(F32)
            acc[b, z_ * 128:(z_ + 1) * 128, :] = total_piece
        lzs[b] = acc[b, pl.ds(pl.multiple_of(oz * 128, 128), 128), :].astype(BF16)
        remote(lzs.at[b], lzr.at[b], lz_send.at[b], lz_recv.at[b], zdev).start()
    for h in range(NH):
        stagez(h).wait_recv()
        out = fsum[h] + rz[h].astype(F32)
        cols = slice(h * HD, (h + 1) * HD)
        gk_out[:, cols] = out[0:64, 0:HD]
        gv_out[:, cols] = out[0:64, HD:2 * HD]
        gq_out[0:16, cols] = out[64:80, 0:HD]
        gq_out[16:32, cols] = out[64:80, HD:2 * HD]
    for b in range(2):
        copy = remote(lzs.at[b], lzr.at[b], lz_send.at[b], lz_recv.at[b], zdev)
        copy.wait_recv()
        mine = pl.ds(pl.multiple_of(zh * 128, 128), 128)
        gl_out[:, b * 256:(b + 1) * 256] = acc[b, mine, :] + lzr[b].astype(F32)
        copy.wait_send()

    for k in range(8):
        for index, device in arrivals[k][1]:
            ag(index, arrivals[k][0], device, own_ref if k == 0 else None).wait_send()
    for d in range(1, 8):
        stat(d, ci).wait_send()
    for h in range(NH):
        s = 1 if h % 2 == 0 else 3
        stage1(h, s).wait_send()
        direct(h, s).wait_send()
        stage2(h, s).wait_send()
        stagez(h).wait_send()
    for d in range(4):
        pairwise(d).wait_send()
    for b, s in DIRS:
        ycopy(b, 0, s).wait_send()
        ycopy(b, 1, 4 - s).wait_send()
        ycopy(b, 2, s).wait_send()


def local(queries, grad_out, latent, up_key, up_value):
    dma = pltpu.SemaphoreType.DMA
    vmem = pltpu.VMEM
    full = pl.BlockSpec(memory_space=pltpu.VMEM)
    shape = jax.ShapeDtypeStruct
    return pl.pallas_call(
        kernel,
        out_shape=(
            shape((32, 1024), F32), shape((128, 512), F32),
            shape((64, 1024), F32), shape((64, 1024), F32),
        ),
        in_specs=[full] * 5,
        out_specs=(full,) * 4,
        scratch_shapes=[
            vmem((ROWS, 512), BF16), vmem((512, ROWS), BF16), vmem((2048, 512), BF16),
            vmem((NH, HD, NQ), BF16), vmem((NH, HD, NQ), BF16),
            vmem((ROWS, 2048), BF16), vmem((NH, ROWS, NQ), F32), vmem((NH, ROWS, NQ), F32),
            vmem((TILE, NQ), F32),
            vmem((NH, 8, NQ), F32), vmem((NH, 8, NQ), F32), vmem((NH, 8, NQ), F32),
            vmem((8, 3 * NH, NQ), F32), vmem((NH, 8, NQ), F32), vmem((NH, NQ), F32),
            vmem((2, 256, 256), F32),
            vmem((NH, 4, 2, 80, 256), BF16),
            vmem((NH, 2, 80, 256), BF16), vmem((NH, 2, 80, 256), BF16), vmem((NH, 2, 80, 256), BF16),
            vmem((NH, 80, 256), BF16), vmem((NH, 80, 256), BF16), vmem((NH, 80, 256), F32),
            vmem((4, 2, 2, 128, 256), BF16), vmem((4, 2, 2, 128, 256), BF16),
            vmem((2, 3, 2, 128, 256), BF16), vmem((2, 3, 2, 128, 256), BF16),
            vmem((2, 128, 256), BF16), vmem((2, 128, 256), BF16),
            dma((15,)), dma((16,)), dma((7,)), dma((8,)),
            dma((NH,)), dma((NH,)), dma((NH,)), dma((NH,)),
            dma((NH,)), dma((NH,)), dma((NH,)), dma((NH,)),
            dma((4,)), dma((4,)), dma((2, 3)), dma((2, 3)), dma((2,)), dma((2,)),
        ],
        compiler_params=pltpu.CompilerParams(
            collective_id=0, has_side_effects=True, vmem_limit_bytes=67043328
        ),
    )(queries, grad_out, latent, up_key, up_value)


def solution(mesh):
    return jax.shard_map(
        local,
        mesh=mesh,
        in_specs=(
            P(None, "head"),
            P(None, "head"),
            P(("ctx", "head"), None),
            P(None, "head"),
            P(None, "head"),
        ),
        out_specs=(P("ctx", "head"), P(("ctx", "head"), None), P("ctx", "head"), P("ctx", "head")),
        check_vma=False,
    )
```

```python
import math

import jax
import jax.numpy as jnp
from jax import lax
from jax.experimental import pallas as pl
from jax.experimental.pallas import tpu as pltpu
from jax.sharding import PartitionSpec as P

HD = 128
NH = 8
ROWS = 2048
TILE = 256
NQ = 256
NEG = -1e30
F32 = jnp.float32
BF16 = jnp.bfloat16
MESH = pl.DeviceIdType.MESH
SCALE = 1.0 / math.sqrt(HD)
SCALE2 = SCALE / math.log(2.0)
TN = (((0,), (0,)), ((), ()))


def dot(a, b):
    return jnp.dot(a, b, preferred_element_type=F32)


def kernel(
    q_hbm, go_hbm, own_hbm, upk_hbm, upv_hbm,
    gq_out, gl_out, gk_out, gv_out,
    q_ref, go_ref, upk_ref, upv_ref,
    lat, lat_t, up_t, q_t, go_t, kk, ebuf, gbuf, bias,
    mst, tst, dst, st_all, wst, delta, acc,
    pbuf, rbuf, gds, gdr, ls, lr, held, lpart,
    in_sem, ag_send, ag_recv, st_send, st_recv, up_send, up_recv,
    gd_send, gd_recv, l_send, l_recv,
):
    ci = lax.axis_index("ctx")
    hi = lax.axis_index("head")
    x, zl = ci // 2, ci % 2
    zh, y, core = hi // 8, (hi // 2) % 4, hi % 2
    oz = 1 - zh

    def ym(d):
        return (y + d) % 4

    def xm(d):
        return (x + d) % 4

    partner = (ci, zh * 8 + y * 2 + 1 - core)
    peers = [((ci + d) % 8, hi) for d in range(1, 8)]

    def chip(z_, d):
        if z_ == 0:
            return (ci, zh * 8 + ym(d) * 2 + core)
        return (x * 2 + 1 - zl, oz * 8 + ym(d) * 2 + core)

    def slot(z_, y_, c_):
        return z_ * 8 + y_ * 2 + c_

    def slot_rows(s):
        return lat.at[pl.ds(pl.multiple_of(s * 128, 128), 128), :]

    own_slot = slot(zh, y, core)
    loads = [
        pltpu.make_async_copy(src, dst, in_sem.at[i])
        for i, (src, dst) in enumerate((
            (own_hbm, slot_rows(own_slot)), (q_hbm, q_ref), (go_hbm, go_ref),
            (upk_hbm, upk_ref), (upv_hbm, upv_ref),
        ))
    ]
    for load in loads:
        load.start()

    order = ((1, 0), (0, 3), (0, 1), (1, 3), (1, 1), (0, 2), (1, 2))
    barrier = pltpu.get_barrier_semaphore()
    for d in [partner] + [chip(z_, d) for z_, d in order] + peers:
        pl.semaphore_signal(barrier, inc=1, device_id=d, device_id_type=MESH)

    def remote(src, dst, ss, rs, device):
        return pltpu.make_async_remote_copy(
            src_ref=src, dst_ref=dst, send_sem=ss, recv_sem=rs,
            device_id=device, device_id_type=MESH,
        )

    def ag(index, s, device):
        return remote(slot_rows(s), slot_rows(s), ag_send.at[index], ag_recv.at[s], device)

    slots = [own_slot] + [slot(zh if z_ == 0 else oz, ym(d), core) for z_, d in order]

    def outgoing(k):
        z_, d = order[k - 1]
        return ag(k, own_slot, chip(z_, (4 - d) % 4))

    def forward(k):
        return ag(7 + k, slots[k], partner)

    loads[0].wait()
    pl.semaphore_wait(barrier, 15)
    ag(0, own_slot, partner).start()
    for k in range(1, 4):
        outgoing(k).start()
    for load in loads[1:]:
        load.wait()

    for h in range(NH):
        cols = slice(h * HD, (h + 1) * HD)
        q_t[h] = q_ref[:, cols].T
        go_t[h] = go_ref[:, cols].T

    last_owner = jnp.logical_and(x == 3, zl == zh)
    key_row = lax.broadcasted_iota(jnp.int32, (TILE, NQ), 0)
    query_col = lax.broadcasted_iota(jnp.int32, (TILE, NQ), 1)

    @pl.loop(0, 8)
    def _(step):
        @pl.when(step == 1)
        def _():
            outgoing(4).start()
            outgoing(5).start()

        for k in range(1, 8):
            @pl.when(step == max(k - 1, 1))
            def _(k=k):
                ag(k, slots[k], partner).wait_recv()
                forward(k).start()
                if k == 1:
                    outgoing(6).start()
                    outgoing(7).start()
        for k in range(8):
            @pl.when(step == k)
            def _(k=k):
                ag(0, slots[k] + 1 - 2 * core, partner).wait_recv()
        y_t = (y + jnp.where(step < 2, 0, jnp.where(step >= 6, 2, jnp.where(step % 2 == 0, 3, 1)))) % 4
        z_t = (zh + jnp.where(step < 4, jnp.where(step == 1, 1, 0), jnp.where(step == 6, 0, 1))) % 2
        t = z_t * 4 + y_t
        rows = pl.ds(pl.multiple_of(t * TILE, TILE), TILE)
        limit = jnp.where(jnp.logical_and(last_owner, t == 7), 0, 4 * TILE)
        bias[...] = jnp.where(key_row > query_col + limit, NEG, 0.0)
        block = lat[rows, :]
        lat_t[:, rows] = block.T
        for pair in range(NH // 2):
            cols = slice(pair * 2 * HD, (pair + 1) * 2 * HD)
            k2 = dot(block, upk_ref[:, cols])
            v2 = dot(block, upv_ref[:, cols]).astype(BF16)
            for b in range(2):
                h = pair * 2 + b
                half = slice(b * HD, (b + 1) * HD)
                key = k2[:, half]
                key_hi = key.astype(BF16)
                key_lo = (key - key_hi.astype(F32)).astype(BF16)
                both = jnp.concatenate([key_hi, key_lo], axis=1)
                kk[rows, h * 256:(h + 1) * 256] = both
                qt = q_t[h]
                s = dot(both, jnp.concatenate([qt, qt], axis=0)) + bias[...]
                g = dot(v2[:, half], go_t[h])
                m = jnp.max(s, axis=0, keepdims=True)
                e = jnp.exp2((s - m) * SCALE2)
                ebuf[h, rows, :] = e
                gbuf[h, rows, :] = g
                mst[h, pl.ds(t, 1), :] = m
                tst[h, pl.ds(t, 1), :] = jnp.sum(e, axis=0, keepdims=True)
                dst[h, pl.ds(t, 1), :] = jnp.sum(e * g, axis=0, keepdims=True)

    for h in range(NH):
        mt = mst[h]
        m = jnp.max(mt, axis=0, keepdims=True)
        w = jnp.exp2((mt - m) * SCALE2)
        st_all[ci, h:h + 1, :] = m
        st_all[ci, NH + h:NH + h + 1, :] = jnp.sum(w * tst[h], axis=0, keepdims=True)
        st_all[ci, 2 * NH + h:2 * NH + h + 1, :] = jnp.sum(w * dst[h], axis=0, keepdims=True)

    def stat(d, index):
        return remote(st_all.at[index], st_all.at[index], st_send.at[d - 1], st_recv.at[index], peers[d - 1])

    for d in range(1, 8):
        stat(d, ci).start()
    @pl.loop(0, NH)
    def _(h):
        cols = pl.ds(pl.multiple_of(h * HD, HD), HD)
        rows = pl.multiple_of(h * 2 * HD, 2 * HD)
        up_t[pl.ds(rows, HD), :] = upk_ref[:, cols].T
        up_t[pl.ds(rows + HD, HD), :] = upv_ref[:, cols].T

    for d in range(1, 8):
        stat(d, (ci + d) % 8).wait_recv()
    m_all = st_all[0, 0:NH, :]
    for c in range(1, 8):
        m_all = jnp.maximum(m_all, st_all[c, 0:NH, :])
    total = jnp.zeros((NH, NQ), F32)
    product = jnp.zeros((NH, NQ), F32)
    for c in range(8):
        w = jnp.exp2((st_all[c, 0:NH, :] - m_all) * SCALE2)
        total += w * st_all[c, NH:2 * NH, :]
        product += w * st_all[c, 2 * NH:3 * NH, :]
    delta[...] = product / total
    inverse = 1.0 / total
    for h in range(NH):
        wst[h] = jnp.exp2((mst[h] - m_all[h:h + 1]) * SCALE2) * inverse[h:h + 1]

    def up_copy(h, d):
        return remote(
            pbuf.at[h, (ci + d) % 8], rbuf.at[h, d - 1], up_send.at[h, d - 1], up_recv.at[h, d - 1], peers[d - 1]
        )

    def head_tile(h, t):
        rows = pl.ds(pl.multiple_of(t * TILE, TILE), TILE)
        hcols = pl.ds(pl.multiple_of(h * HD, HD), HD)
        kcols = pl.ds(pl.multiple_of(h * 256, 256), 256)
        prob = ebuf[h, rows, :] * wst[h, pl.ds(t, 1), :]
        gs = (prob * (gbuf[h, rows, :] - delta[pl.ds(h, 1), :]) * SCALE).astype(BF16)
        acc[...] += lax.dot_general(gs, kk[rows, kcols], TN, preferred_element_type=F32)
        gk = dot(gs, q_ref[:, hcols]).astype(BF16)
        gv = dot(prob.astype(BF16), go_ref[:, hcols]).astype(BF16)
        kk[rows, kcols] = jnp.concatenate([gk, gv], axis=1)

    def head_sums(h):
        kcols = pl.ds(pl.multiple_of(h * 256, 256), 256)
        gq = acc[:, 0:HD] + acc[:, HD:2 * HD]
        up = dot(lat_t[...], kk[:, kcols]).astype(BF16)
        for c in range(8):
            pbuf[h, c, 0:64, :] = up[c * 64:c * 64 + 64, :]
            pbuf[h, c, 64:80, :] = jnp.concatenate(
                [gq[c * 32:c * 32 + 16], gq[c * 32 + 16:c * 32 + 32]], axis=1
            ).astype(BF16)
        for d in (4, 3, 5, 2, 6, 1, 7):
            up_copy(h, d).start()

    @pl.loop(0, NH - 1)
    def _(h):
        acc[...] = jnp.zeros_like(acc)
        for t in range(8):
            head_tile(h, t)
        head_sums(h)

    sends = ((1, 2), (0, 2), (1, 1), (1, 3), (0, 1), (0, 3), (1, 0), (0, 0))
    mine = pl.ds(pl.multiple_of(core * 128, 128), 128)
    theirs = pl.ds(pl.multiple_of((1 - core) * 128, 128), 128)

    def pairwise(i):
        return remote(gds.at[i], gdr.at[i], gd_send.at[i], gd_recv.at[i], partner)

    def latent_tile(i):
        z_, d = sends[i]
        t = (zh if z_ == 0 else oz) * 4 + ym(d)
        head_tile(NH - 1, t)
        part = dot(kk[pl.ds(pl.multiple_of(t * TILE, TILE), TILE), :], up_t[...])
        lpart[i % 2] = part
        gds[i] = lpart[i % 2, theirs, :].astype(BF16)
        pairwise(i).start()
        held[i] = lpart[i % 2, mine, :]

    def lat_copy(i):
        return remote(ls.at[i], lr.at[i], l_send.at[i], l_recv.at[i], chip(*sends[i]))

    def lat_send(i):
        pairwise(i).wait_recv()
        ls[i] = (held[i] + gdr[i].astype(F32)).astype(BF16)
        lat_copy(i).start()

    acc[...] = jnp.zeros_like(acc)
    for i in range(8):
        latent_tile(i)
        if i >= 2:
            lat_send(i - 2)
    lat_send(6)
    head_sums(NH - 1)
    for h in range(NH):
        for d in range(1, 8):
            up_copy(h, d).wait_recv()
        out = pbuf[h, ci].astype(F32)
        for d in range(7):
            out += rbuf[h, d].astype(F32)
        cols = slice(h * HD, (h + 1) * HD)
        gk_out[:, cols] = out[0:64, 0:HD]
        gv_out[:, cols] = out[0:64, HD:2 * HD]
        gq_out[0:16, cols] = out[64:80, 0:HD]
        gq_out[16:32, cols] = out[64:80, HD:2 * HD]
    pairwise(7).wait_recv()
    out = held[7] + gdr[7].astype(F32)
    for i in range(7):
        lat_copy(i).wait_recv()
        out += lr[i].astype(F32)
    gl_out[...] = out

    ag(0, own_slot, partner).wait_send()
    for k in range(1, 8):
        outgoing(k).wait_send()
        forward(k).wait_send()
    for d in range(1, 8):
        stat(d, ci).wait_send()
        for h in range(NH):
            up_copy(h, d).wait_send()
    for i in range(8):
        pairwise(i).wait_send()
    for i in range(7):
        lat_copy(i).wait_send()


def settle(*refs):
    for source, result in zip(refs[:4], refs[4:]):
        result[...] = source[...]


def local(queries, grad_out, latent, up_key, up_value):
    dma = pltpu.SemaphoreType.DMA
    vmem = pltpu.VMEM
    full = pl.BlockSpec(memory_space=pltpu.VMEM)
    place = pl.BlockSpec(memory_space=pl.ANY)
    shape = jax.ShapeDtypeStruct
    results = (
        shape((32, 1024), F32), shape((128, 512), F32),
        shape((64, 1024), F32), shape((64, 1024), F32),
    )
    sums = pl.pallas_call(
        kernel,
        out_shape=results,
        in_specs=[place] * 5,
        out_specs=(full,) * 4,
        scratch_shapes=[
            vmem((NQ, 1024), BF16), vmem((NQ, 1024), BF16), vmem((512, 1024), BF16), vmem((512, 1024), BF16),
            vmem((ROWS, 512), BF16), vmem((512, ROWS), BF16), vmem((2048, 512), BF16),
            vmem((NH, HD, NQ), BF16), vmem((NH, HD, NQ), BF16),
            vmem((ROWS, 2048), BF16), vmem((NH, ROWS, NQ), F32), vmem((NH, ROWS, NQ), F32),
            vmem((TILE, NQ), F32),
            vmem((NH, 8, NQ), F32), vmem((NH, 8, NQ), F32), vmem((NH, 8, NQ), F32),
            vmem((8, 3 * NH, NQ), F32), vmem((NH, 8, NQ), F32), vmem((NH, NQ), F32),
            vmem((256, 256), F32),
            vmem((NH, 8, 80, 256), BF16), vmem((NH, 7, 80, 256), BF16),
            vmem((8, 128, 512), BF16), vmem((8, 128, 512), BF16), vmem((7, 128, 512), BF16), vmem((7, 128, 512), BF16),
            vmem((8, 128, 512), F32), vmem((2, 256, 512), F32),
            dma((5,)), dma((15,)), dma((16,)), dma((7,)), dma((8,)), dma((NH, 7)), dma((NH, 7)),
            dma((8,)), dma((8,)), dma((7,)), dma((7,)),
        ],
        compiler_params=pltpu.CompilerParams(
            collective_id=0, has_side_effects=True, vmem_limit_bytes=67043328
        ),
    )(queries, grad_out, latent, up_key, up_value)
    return pl.pallas_call(settle, out_shape=results, in_specs=[full] * 4, out_specs=(full,) * 4)(*sums)


def solution(mesh):
    return jax.shard_map(
        local,
        mesh=mesh,
        in_specs=(
            P(None, "head"),
            P(None, "head"),
            P(("ctx", "head"), None),
            P(None, "head"),
            P(None, "head"),
        ),
        out_specs=(P("ctx", "head"), P(("ctx", "head"), None), P("ctx", "head"), P("ctx", "head")),
        check_vma=False,
    )
```

```python
import math

import jax
import jax.numpy as jnp
from jax import lax
from jax.experimental import pallas as pl
from jax.experimental.pallas import tpu as pltpu
from jax.sharding import PartitionSpec as P

HD = 128
NH = 8
ROWS = 2048
TILE = 256
NQ = 256
NEG = -1e30
F32 = jnp.float32
BF16 = jnp.bfloat16
MESH = pl.DeviceIdType.MESH
SCALE = 1.0 / math.sqrt(HD)
SCALE2 = SCALE / math.log(2.0)
TN = (((0,), (0,)), ((), ()))


def dot(a, b):
    return jnp.dot(a, b, preferred_element_type=F32)


def kernel(
    q_hbm, go_hbm, own_hbm, upk_hbm, upv_hbm,
    gq_out, gl_out, gk_out, gv_out,
    q_ref, go_ref, upk_ref, upv_ref,
    lat, lat_t, up_t, q_t, go_t, kk, ebuf, gbuf, bias,
    mst, tst, dst, st_all, wst, delta, acc,
    pbuf, rbuf, gds, gdr, ls, lr,
    in_sem, ag_send, ag_recv, st_send, st_recv, up_send, up_recv,
    gd_send, gd_recv, l_send, l_recv,
):
    ci = lax.axis_index("ctx")
    hi = lax.axis_index("head")
    x, zl = ci // 2, ci % 2
    zh, y, core = hi // 8, (hi // 2) % 4, hi % 2
    oz = 1 - zh

    def ym(d):
        return (y + d) % 4

    def xm(d):
        return (x + d) % 4

    partner = (ci, zh * 8 + y * 2 + 1 - core)
    peers = [((ci + d) % 8, hi) for d in range(1, 8)]

    def chip(z_, d):
        if z_ == 0:
            return (ci, zh * 8 + ym(d) * 2 + core)
        return (x * 2 + 1 - zl, oz * 8 + ym(d) * 2 + core)

    def slot(z_, y_, c_):
        return z_ * 8 + y_ * 2 + c_

    def slot_rows(s):
        return lat.at[pl.ds(pl.multiple_of(s * 128, 128), 128), :]

    own_slot = slot(zh, y, core)
    loads = [
        pltpu.make_async_copy(src, dst, in_sem.at[i])
        for i, (src, dst) in enumerate((
            (own_hbm, slot_rows(own_slot)), (q_hbm, q_ref), (go_hbm, go_ref),
            (upk_hbm, upk_ref), (upv_hbm, upv_ref),
        ))
    ]
    for load in loads:
        load.start()

    order = ((1, 0), (0, 3), (0, 1), (1, 3), (0, 2), (1, 1), (1, 2))
    barrier = pltpu.get_barrier_semaphore()
    for d in [partner] + [chip(z_, d) for z_, d in order] + peers:
        pl.semaphore_signal(barrier, inc=1, device_id=d, device_id_type=MESH)

    def remote(src, dst, ss, rs, device):
        return pltpu.make_async_remote_copy(
            src_ref=src, dst_ref=dst, send_sem=ss, recv_sem=rs,
            device_id=device, device_id_type=MESH,
        )

    def ag(index, s, device):
        return remote(slot_rows(s), slot_rows(s), ag_send.at[index], ag_recv.at[s], device)

    slots = [own_slot] + [slot(zh if z_ == 0 else oz, ym(d), core) for z_, d in order]

    def outgoing(k):
        z_, d = order[k - 1]
        return ag(k, own_slot, chip(z_, (4 - d) % 4))

    def forward(k):
        return ag(7 + k, slots[k], partner)

    loads[0].wait()
    pl.semaphore_wait(barrier, 15)
    ag(0, own_slot, partner).start()
    for k in range(1, 4):
        outgoing(k).start()
    for load in loads[1:]:
        load.wait()

    for h in range(NH):
        cols = slice(h * HD, (h + 1) * HD)
        q_t[h] = q_ref[:, cols].T
        go_t[h] = go_ref[:, cols].T

    last_owner = jnp.logical_and(x == 3, zl == zh)
    key_row = lax.broadcasted_iota(jnp.int32, (TILE, NQ), 0)
    query_col = lax.broadcasted_iota(jnp.int32, (TILE, NQ), 1)

    def receive(k):
        ag(k, slots[k], partner).wait_recv()
        forward(k).start()

    def from_partner(k):
        ag(0, slots[k] + 1 - 2 * core, partner).wait_recv()

    def score_tile(step, base, pairs):
        odd = step % 2
        y_t = (y + jnp.where(step < 2, 0, jnp.where(step < 5, 3 - 2 * odd, 1 + odd))) % 4
        z_t = (zh + jnp.where(step < 4, jnp.where(step == 1, 1, 0), jnp.where(step == 5, 0, 1))) % 2
        t = z_t * 4 + y_t
        rows = pl.ds(pl.multiple_of(t * TILE, TILE), TILE)
        limit = jnp.where(jnp.logical_and(last_owner, t == 7), 0, 4 * TILE)
        bias[...] = jnp.where(key_row > query_col + limit, NEG, 0.0)
        block = lat[rows, :]
        lat_t[:, rows] = block.T

        def project(pair):
            first = base + pair * 2
            cols = pl.ds(first * HD, 2 * HD) if isinstance(first, int) else pl.ds(pl.multiple_of(first * HD, 2 * HD), 2 * HD)
            k2 = dot(block, upk_ref[:, cols])
            v2 = dot(block, upv_ref[:, cols]).astype(BF16)
            parts = []
            for b in range(2):
                half = slice(b * HD, (b + 1) * HD)
                key = k2[:, half]
                key_hi = key.astype(BF16)
                key_lo = (key - key_hi.astype(F32)).astype(BF16)
                both = jnp.concatenate([key_hi, key_lo], axis=1)
                start = (first + b) * 256
                kcols = pl.ds(start, 256) if isinstance(start, int) else pl.ds(pl.multiple_of(start, 256), 256)
                kk[rows, kcols] = both
                parts.append((both, v2[:, half]))
            return parts

        def score(pair, parts):
            for b in range(2):
                h = base + pair * 2 + b
                qt = q_t[h]
                s = dot(parts[b][0], jnp.concatenate([qt, qt], axis=0)) + bias[...]
                g = dot(parts[b][1], go_t[h])
                m = jnp.max(s, axis=0, keepdims=True)
                e = jnp.exp2((s - m) * SCALE2)
                ebuf[h, rows, :] = e
                gbuf[h, rows, :] = g
                mst[h, pl.ds(t, 1), :] = m
                tst[h, pl.ds(t, 1), :] = jnp.sum(e, axis=0, keepdims=True)
                dst[h, pl.ds(t, 1), :] = jnp.sum(e * g, axis=0, keepdims=True)

        pending = project(0)
        for pair in range(pairs):
            following = project(pair + 1) if pair + 1 < pairs else None
            score(pair, pending)
            pending = following

    def stat(g, d, index):
        place = st_all.at[g, index]
        return remote(place, place, st_send.at[g, d - 1], st_recv.at[g, index], peers[d - 1])

    def stats_send(g):
        for i in range(NH):
            h = g * NH + i
            mt = mst[h]
            m = jnp.max(mt, axis=0, keepdims=True)
            w = jnp.exp2((mt - m) * SCALE2)
            st_all[g, ci, i:i + 1, :] = m
            st_all[g, ci, NH + i:NH + i + 1, :] = jnp.sum(w * tst[h], axis=0, keepdims=True)
            st_all[g, ci, 2 * NH + i:2 * NH + i + 1, :] = jnp.sum(w * dst[h], axis=0, keepdims=True)
        for d in range(1, 8):
            stat(g, d, ci).start()

    def stats_join(g):
        for d in range(1, 8):
            stat(g, d, (ci + d) % 8).wait_recv()
        half = NH
        m_all = st_all[g, 0, 0:half, :]
        for c in range(1, 8):
            m_all = jnp.maximum(m_all, st_all[g, c, 0:half, :])
        total = jnp.zeros((half, NQ), F32)
        product = jnp.zeros((half, NQ), F32)
        for c in range(8):
            w = jnp.exp2((st_all[g, c, 0:half, :] - m_all) * SCALE2)
            total += w * st_all[g, c, NH:NH + half, :]
            product += w * st_all[g, c, 2 * NH:2 * NH + half, :]
        delta[g * half:(g + 1) * half, :] = product / total
        inverse = 1.0 / total
        for i in range(half):
            h = g * half + i
            wst[h] = jnp.exp2((mst[h] - m_all[i:i + 1]) * SCALE2) * inverse[i:i + 1]

    @pl.loop(0, 8)
    def _(step):
        for k in range(1, 8):
            @pl.when(step == max(k - 1, 1))
            def _(k=k):
                if k == 1:
                    outgoing(4).start()
                    outgoing(5).start()
                receive(k)
                if k == 1:
                    outgoing(6).start()
                    outgoing(7).start()
        for k in range(8):
            @pl.when(step == k)
            def _(k=k):
                from_partner(k)
        score_tile(step, 0, NH // 2)

    stats_send(0)

    @pl.loop(0, NH)
    def _(h):
        cols = pl.ds(pl.multiple_of(h * HD, HD), HD)
        rows = pl.multiple_of(h * 2 * HD, 2 * HD)
        up_t[pl.ds(rows, HD), :] = upk_ref[:, cols].T
        up_t[pl.ds(rows + HD, HD), :] = upv_ref[:, cols].T

    stats_join(0)

    zpeer = (x * 2 + 1 - zl, hi)
    kinds = (0, 1, 0, 1, 0, 1, 2, 2)
    straight = ((2, 1), (2, 0), (1, 1), (3, 1), (1, 0), (3, 0), (0, 1))

    def up_copy(h, j, src, dst, device):
        return remote(src, dst, up_send.at[h, j], up_recv.at[h, j], device)

    def first_copies(kind, h):
        if kind == 0:
            return [
                up_copy(h, d - 1, pbuf.at[h, xm(d)], rbuf.at[h, pl.ds(2 * d - 2, 2)], (xm(d) * 2 + zl, hi))
                for d in (2, 1, 3)
            ]
        if kind == 1:
            return [up_copy(h, 0, pbuf.at[h, :, 1 - zl], rbuf.at[h, pl.ds(0, 4)], zpeer)]
        return [
            up_copy(h, j, pbuf.at[h, xm(d), (zl + z_) % 2], rbuf.at[h, j], (xm(d) * 2 + (zl + z_) % 2, hi))
            for j, (d, z_) in enumerate(straight)
        ]

    def second_copies(kind, h):
        if kind == 0:
            return [up_copy(h, 3, pbuf.at[h, x, 1 - zl], rbuf.at[h, 6], zpeer)]
        if kind == 1:
            return [
                up_copy(h, d, pbuf.at[h, xm(d), zl], rbuf.at[h, 3 + d], (xm(d) * 2 + zl, hi)) for d in (2, 1, 3)
            ]
        return []

    def pass_on(h):
        kind = kinds[h]
        for copy in first_copies(kind, h):
            copy.wait_recv()
        if kind == 0:
            part = pbuf[h, x, 1 - zl].astype(F32)
            for d in range(3):
                part += rbuf[h, 2 * d + 1 - zl].astype(F32)
            pbuf[h, x, 1 - zl] = part.astype(BF16)
        else:
            for d in range(1, 4):
                pbuf[h, xm(d), zl] = (pbuf[h, xm(d), zl].astype(F32) + rbuf[h, xm(d)].astype(F32)).astype(BF16)
        for copy in second_copies(kind, h):
            copy.start()

    def up_result(h):
        kind = kinds[h]
        for copy in second_copies(kind, h) if kind < 2 else first_copies(kind, h):
            copy.wait_recv()
        out = pbuf[h, x, zl].astype(F32)
        if kind == 0:
            pieces = [2 * d + zl for d in range(3)] + [6]
        elif kind == 1:
            pieces = [x, 4, 5, 6]
        else:
            pieces = list(range(7))
        for piece in pieces:
            out += rbuf[h, piece].astype(F32)
        return out

    def head_tile(h, t):
        rows = pl.ds(pl.multiple_of(t * TILE, TILE), TILE)
        hcols = pl.ds(pl.multiple_of(h * HD, HD), HD)
        kcols = pl.ds(pl.multiple_of(h * 256, 256), 256)
        prob = ebuf[h, rows, :] * wst[h, pl.ds(t, 1), :]
        gs = (prob * (gbuf[h, rows, :] - delta[pl.ds(h, 1), :]) * SCALE).astype(BF16)
        acc[...] += lax.dot_general(gs, kk[rows, kcols], TN, preferred_element_type=F32)
        gk = dot(gs, q_ref[:, hcols]).astype(BF16)
        gv = dot(prob.astype(BF16), go_ref[:, hcols]).astype(BF16)
        kk[rows, kcols] = jnp.concatenate([gk, gv], axis=1)

    def head_sums(h):
        kcols = pl.ds(pl.multiple_of(h * 256, 256), 256)
        gq = acc[:, 0:HD] + acc[:, HD:2 * HD]
        up = dot(lat_t[...], kk[:, kcols]).astype(BF16)
        for c in range(8):
            pbuf[h, c // 2, c % 2, 0:64, :] = up[c * 64:c * 64 + 64, :]
            pbuf[h, c // 2, c % 2, 64:80, :] = jnp.concatenate(
                [gq[c * 32:c * 32 + 16], gq[c * 32 + 16:c * 32 + 32]], axis=1
            ).astype(BF16)

    def launch(kind, h):
        for copy in first_copies(kind, h):
            copy.start()

    @pl.loop(0, NH - 1)
    def _(h):
        acc[...] = jnp.zeros_like(acc)
        for t in range(8):
            head_tile(h, t)
        head_sums(h)

        @pl.when(jnp.logical_and(h < 6, h % 2 == 0))
        def _():
            launch(0, h)

        @pl.when(jnp.logical_and(h < 6, h % 2 == 1))
        def _():
            launch(1, h)

        @pl.when(h == 5)
        def _():
            pass_on(0)

        @pl.when(h == 6)
        def _():
            launch(2, h)
            pass_on(1)

    sends = ((1, 2), (0, 2), (1, 1), (1, 3), (0, 1), (0, 3), (1, 0), (0, 0))

    def pairwise(i):
        return remote(gds.at[i], gdr.at[i], gd_send.at[i], gd_recv.at[i], partner)

    def latent_tile(i):
        z_, d = sends[i]
        t = (zh if z_ == 0 else oz) * 4 + ym(d)
        part = dot(kk[pl.ds(pl.multiple_of(t * TILE, TILE), TILE), :], up_t[...])
        for b in range(2):
            cols = slice(b * 256, (b + 1) * 256)
            ebuf[i, b * 256:(b + 1) * 256, :] = part[:, cols]
            gds[i, :, cols] = ebuf[i, pl.ds(pl.multiple_of(b * 256 + (1 - core) * 128, 128), 128), :].astype(BF16)
        pairwise(i).start()

    def held(i, b):
        rows = pl.ds(pl.multiple_of(b * 256 + core * 128, 128), 128)
        return ebuf[i, rows, :] + gdr[i, :, b * 256:(b + 1) * 256].astype(F32)

    def lat_copy(i):
        return remote(ls.at[i], lr.at[i], l_send.at[i], l_recv.at[i], chip(*sends[i]))

    def lat_send(i):
        pairwise(i).wait_recv()
        for b in range(2):
            ls[i, :, b * 256:(b + 1) * 256] = held(i, b).astype(BF16)
        lat_copy(i).start()

    acc[...] = jnp.zeros_like(acc)
    for t in range(8):
        head_tile(NH - 1, t)
    for i in range(8):
        latent_tile(i)
        if i >= 2:
            lat_send(i - 2)
        if i == 3:
            head_sums(NH - 1)
            launch(2, NH - 1)
        if i % 2 == 0:
            pass_on(2 + i // 2)
    lat_send(6)
    for h in range(NH):
        out = up_result(h)
        cols = slice(h * HD, (h + 1) * HD)
        gk_out[:, cols] = out[0:64, 0:HD]
        gv_out[:, cols] = out[0:64, HD:2 * HD]
        gq_out[0:16, cols] = out[64:80, 0:HD]
        gq_out[16:32, cols] = out[64:80, HD:2 * HD]
    pairwise(7).wait_recv()
    for i in range(7):
        lat_copy(i).wait_recv()
    for b in range(2):
        out = held(7, b)
        for i in range(7):
            out += lr[i, :, b * 256:(b + 1) * 256].astype(F32)
        gl_out[:, b * 256:(b + 1) * 256] = out

    ag(0, own_slot, partner).wait_send()
    for k in range(1, 8):
        outgoing(k).wait_send()
        forward(k).wait_send()
    for d in range(1, 8):
        stat(0, d, ci).wait_send()
    for h in range(NH):
        for copy in first_copies(kinds[h], h) + second_copies(kinds[h], h):
            copy.wait_send()
    for i in range(8):
        pairwise(i).wait_send()
    for i in range(7):
        lat_copy(i).wait_send()


def settle(*refs):
    for source, result in zip(refs[:4], refs[4:]):
        result[...] = source[...]


def local(queries, grad_out, latent, up_key, up_value):
    dma = pltpu.SemaphoreType.DMA
    vmem = pltpu.VMEM
    full = pl.BlockSpec(memory_space=pltpu.VMEM)
    place = pl.BlockSpec(memory_space=pl.ANY)
    shape = jax.ShapeDtypeStruct
    results = (
        shape((32, 1024), F32), shape((128, 512), F32),
        shape((64, 1024), F32), shape((64, 1024), F32),
    )
    sums = pl.pallas_call(
        kernel,
        out_shape=results,
        in_specs=[place] * 5,
        out_specs=(full,) * 4,
        scratch_shapes=[
            vmem((NQ, 1024), BF16), vmem((NQ, 1024), BF16), vmem((512, 1024), BF16), vmem((512, 1024), BF16),
            vmem((ROWS, 512), BF16), vmem((512, ROWS), BF16), vmem((2048, 512), BF16),
            vmem((NH, HD, NQ), BF16), vmem((NH, HD, NQ), BF16),
            vmem((ROWS, 2048), BF16), vmem((NH, ROWS, NQ), F32), vmem((NH, ROWS, NQ), F32),
            vmem((TILE, NQ), F32),
            vmem((NH, 8, NQ), F32), vmem((NH, 8, NQ), F32), vmem((NH, 8, NQ), F32),
            vmem((1, 8, 3 * NH, NQ), F32), vmem((NH, 8, NQ), F32), vmem((NH, NQ), F32),
            vmem((256, 256), F32),
            vmem((NH, 4, 2, 80, 256), BF16), vmem((NH, 7, 80, 256), BF16),
            vmem((8, 128, 512), BF16), vmem((8, 128, 512), BF16), vmem((7, 128, 512), BF16), vmem((7, 128, 512), BF16),
            dma((5,)), dma((15,)), dma((16,)), dma((1, 7)), dma((1, 8)), dma((NH, 7)), dma((NH, 7)),
            dma((8,)), dma((8,)), dma((7,)), dma((7,)),
        ],
        compiler_params=pltpu.CompilerParams(
            collective_id=0, has_side_effects=True, vmem_limit_bytes=67043328
        ),
    )(queries, grad_out, latent, up_key, up_value)
    return pl.pallas_call(settle, out_shape=results, in_specs=[full] * 4, out_specs=(full,) * 4)(*sums)


def solution(mesh):
    return jax.shard_map(
        local,
        mesh=mesh,
        in_specs=(
            P(None, "head"),
            P(None, "head"),
            P(("ctx", "head"), None),
            P(None, "head"),
            P(None, "head"),
        ),
        out_specs=(P("ctx", "head"), P(("ctx", "head"), None), P("ctx", "head"), P("ctx", "head")),
        check_vma=False,
    )
```

```python
import math

import jax
import jax.numpy as jnp
from jax import lax
from jax.experimental import pallas as pl
from jax.experimental.pallas import tpu as pltpu
from jax.sharding import PartitionSpec as P

HD = 128
NH = 8
ROWS = 2048
TILE = 256
NQ = 256
NEG = -1e30
F32 = jnp.float32
BF16 = jnp.bfloat16
MESH = pl.DeviceIdType.MESH
SCALE = 1.0 / math.sqrt(HD)
SCALE2 = SCALE / math.log(2.0)
TN = (((0,), (0,)), ((), ()))


def dot(a, b):
    return jnp.dot(a, b, preferred_element_type=F32)


def kernel(
    q_hbm, go_hbm, own_hbm, upk_hbm, upv_hbm,
    gq_hbm, gl_hbm, gk_hbm, gv_hbm,
    gq_out, gl_out, gk_out, gv_out, out_sem,
    q_ref, go_ref, upk_ref, upv_ref,
    lat, lat_t, up_t, q_t, go_t, kk, ebuf, gbuf, bias,
    mst, tst, dst, st_all, wst, delta, acc,
    pbuf, rbuf, gds, gdr, ls, lr,
    in_sem, ag_send, ag_recv, st_send, st_recv, up_send, up_recv,
    gd_send, gd_recv, l_send, l_recv,
):
    ci = lax.axis_index("ctx")
    hi = lax.axis_index("head")
    x, zl = ci // 2, ci % 2
    zh, y, core = hi // 8, (hi // 2) % 4, hi % 2
    oz = 1 - zh

    def ym(d):
        return (y + d) % 4

    def xm(d):
        return (x + d) % 4

    partner = (ci, zh * 8 + y * 2 + 1 - core)
    peers = [((ci + d) % 8, hi) for d in range(1, 8)]

    def chip(z_, d):
        if z_ == 0:
            return (ci, zh * 8 + ym(d) * 2 + core)
        return (x * 2 + 1 - zl, oz * 8 + ym(d) * 2 + core)

    def slot(z_, y_, c_):
        return z_ * 8 + y_ * 2 + c_

    def slot_rows(s):
        return lat.at[pl.ds(pl.multiple_of(s * 128, 128), 128), :]

    own_slot = slot(zh, y, core)
    loads = [
        pltpu.make_async_copy(src, dst, in_sem.at[i])
        for i, (src, dst) in enumerate((
            (own_hbm, slot_rows(own_slot)), (q_hbm, q_ref), (go_hbm, go_ref),
            (upk_hbm, upk_ref), (upv_hbm, upv_ref),
        ))
    ]
    for load in loads:
        load.start()

    order = ((1, 0), (0, 3), (0, 1), (1, 3), (0, 2), (1, 1), (1, 2))
    barrier = pltpu.get_barrier_semaphore()
    for d in [partner] + [chip(z_, d) for z_, d in order] + peers:
        pl.semaphore_signal(barrier, inc=1, device_id=d, device_id_type=MESH)

    def remote(src, dst, ss, rs, device):
        return pltpu.make_async_remote_copy(
            src_ref=src, dst_ref=dst, send_sem=ss, recv_sem=rs,
            device_id=device, device_id_type=MESH,
        )

    def ag(index, s, device):
        return remote(slot_rows(s), slot_rows(s), ag_send.at[index], ag_recv.at[s], device)

    slots = [own_slot] + [slot(zh if z_ == 0 else oz, ym(d), core) for z_, d in order]

    def outgoing(k):
        z_, d = order[k - 1]
        return ag(k, own_slot, chip(z_, (4 - d) % 4))

    def forward(k):
        return ag(7 + k, slots[k], partner)

    loads[0].wait()
    pl.semaphore_wait(barrier, 15)
    ag(0, own_slot, partner).start()
    for k in range(1, 4):
        outgoing(k).start()
    for load in loads[1:]:
        load.wait()

    for h in range(NH):
        cols = slice(h * HD, (h + 1) * HD)
        q_t[h] = q_ref[:, cols].T
        go_t[h] = go_ref[:, cols].T

    last_owner = jnp.logical_and(x == 3, zl == zh)
    key_row = lax.broadcasted_iota(jnp.int32, (TILE, NQ), 0)
    query_col = lax.broadcasted_iota(jnp.int32, (TILE, NQ), 1)

    def receive(k):
        ag(k, slots[k], partner).wait_recv()
        forward(k).start()

    def from_partner(k):
        ag(0, slots[k] + 1 - 2 * core, partner).wait_recv()

    def score_tile(step, base, pairs):
        odd = step % 2
        y_t = (y + jnp.where(step < 2, 0, jnp.where(step < 5, 3 - 2 * odd, 1 + odd))) % 4
        z_t = (zh + jnp.where(step < 4, jnp.where(step == 1, 1, 0), jnp.where(step == 5, 0, 1))) % 2
        t = z_t * 4 + y_t
        rows = pl.ds(pl.multiple_of(t * TILE, TILE), TILE)
        limit = jnp.where(jnp.logical_and(last_owner, t == 7), 0, 4 * TILE)
        bias[...] = jnp.where(key_row > query_col + limit, NEG, 0.0)
        block = lat[rows, :]
        lat_t[:, rows] = block.T

        def project(pair):
            first = base + pair * 2
            cols = pl.ds(first * HD, 2 * HD) if isinstance(first, int) else pl.ds(pl.multiple_of(first * HD, 2 * HD), 2 * HD)
            k2 = dot(block, upk_ref[:, cols])
            v2 = dot(block, upv_ref[:, cols]).astype(BF16)
            parts = []
            for b in range(2):
                half = slice(b * HD, (b + 1) * HD)
                key = k2[:, half]
                key_hi = key.astype(BF16)
                key_lo = (key - key_hi.astype(F32)).astype(BF16)
                both = jnp.concatenate([key_hi, key_lo], axis=1)
                start = (first + b) * 256
                kcols = pl.ds(start, 256) if isinstance(start, int) else pl.ds(pl.multiple_of(start, 256), 256)
                kk[rows, kcols] = both
                parts.append((both, v2[:, half]))
            return parts

        def score(pair, parts):
            for b in range(2):
                h = base + pair * 2 + b
                qt = q_t[h]
                s = dot(parts[b][0], jnp.concatenate([qt, qt], axis=0)) + bias[...]
                g = dot(parts[b][1], go_t[h])
                m = jnp.max(s, axis=0, keepdims=True)
                e = jnp.exp2((s - m) * SCALE2)
                ebuf[h, rows, :] = e
                gbuf[h, rows, :] = g
                mst[h, pl.ds(t, 1), :] = m
                tst[h, pl.ds(t, 1), :] = jnp.sum(e, axis=0, keepdims=True)
                dst[h, pl.ds(t, 1), :] = jnp.sum(e * g, axis=0, keepdims=True)

        pending = project(0)
        for pair in range(pairs):
            following = project(pair + 1) if pair + 1 < pairs else None
            score(pair, pending)
            pending = following

    def stat(g, d, index):
        place = st_all.at[g, index]
        return remote(place, place, st_send.at[g, d - 1], st_recv.at[g, index], peers[d - 1])

    def stats_send(g):
        for i in range(NH):
            h = g * NH + i
            mt = mst[h]
            m = jnp.max(mt, axis=0, keepdims=True)
            w = jnp.exp2((mt - m) * SCALE2)
            st_all[g, ci, i:i + 1, :] = m
            st_all[g, ci, NH + i:NH + i + 1, :] = jnp.sum(w * tst[h], axis=0, keepdims=True)
            st_all[g, ci, 2 * NH + i:2 * NH + i + 1, :] = jnp.sum(w * dst[h], axis=0, keepdims=True)
        for d in range(1, 8):
            stat(g, d, ci).start()

    def stats_join(g):
        for d in range(1, 8):
            stat(g, d, (ci + d) % 8).wait_recv()
        half = NH
        m_all = st_all[g, 0, 0:half, :]
        for c in range(1, 8):
            m_all = jnp.maximum(m_all, st_all[g, c, 0:half, :])
        total = jnp.zeros((half, NQ), F32)
        product = jnp.zeros((half, NQ), F32)
        for c in range(8):
            w = jnp.exp2((st_all[g, c, 0:half, :] - m_all) * SCALE2)
            total += w * st_all[g, c, NH:NH + half, :]
            product += w * st_all[g, c, 2 * NH:2 * NH + half, :]
        delta[g * half:(g + 1) * half, :] = product / total
        inverse = 1.0 / total
        for i in range(half):
            h = g * half + i
            wst[h] = jnp.exp2((mst[h] - m_all[i:i + 1]) * SCALE2) * inverse[i:i + 1]

    @pl.loop(0, 8)
    def _(step):
        for k in range(1, 8):
            @pl.when(step == max(k - 1, 1))
            def _(k=k):
                if k == 1:
                    outgoing(4).start()
                    outgoing(5).start()
                receive(k)
                if k == 1:
                    outgoing(6).start()
                    outgoing(7).start()
        for k in range(8):
            @pl.when(step == k)
            def _(k=k):
                from_partner(k)
        score_tile(step, 0, NH // 2)

    stats_send(0)

    @pl.loop(0, NH)
    def _(h):
        cols = pl.ds(pl.multiple_of(h * HD, HD), HD)
        rows = pl.multiple_of(h * 2 * HD, 2 * HD)
        up_t[pl.ds(rows, HD), :] = upk_ref[:, cols].T
        up_t[pl.ds(rows + HD, HD), :] = upv_ref[:, cols].T

    stats_join(0)

    zpeer = (x * 2 + 1 - zl, hi)
    kinds = (0, 1, 0, 1, 0, 1, 2, 2)
    straight = ((2, 1), (2, 0), (1, 1), (3, 1), (1, 0), (3, 0), (0, 1))

    def up_copy(h, j, src, dst, device):
        return remote(src, dst, up_send.at[h, j], up_recv.at[h, j], device)

    def first_copies(kind, h):
        if kind == 0:
            return [
                up_copy(h, d - 1, pbuf.at[h, xm(d)], rbuf.at[h, pl.ds(2 * d - 2, 2)], (xm(d) * 2 + zl, hi))
                for d in (2, 1, 3)
            ]
        if kind == 1:
            return [up_copy(h, 0, pbuf.at[h, :, 1 - zl], rbuf.at[h, pl.ds(0, 4)], zpeer)]
        return [
            up_copy(h, j, pbuf.at[h, xm(d), (zl + z_) % 2], rbuf.at[h, j], (xm(d) * 2 + (zl + z_) % 2, hi))
            for j, (d, z_) in enumerate(straight)
        ]

    def second_copies(kind, h):
        if kind == 0:
            return [up_copy(h, 3, pbuf.at[h, x, 1 - zl], rbuf.at[h, 6], zpeer)]
        if kind == 1:
            return [
                up_copy(h, d, pbuf.at[h, xm(d), zl], rbuf.at[h, 3 + d], (xm(d) * 2 + zl, hi)) for d in (2, 1, 3)
            ]
        return []

    def pass_on(h):
        kind = kinds[h]
        for copy in first_copies(kind, h):
            copy.wait_recv()
        if kind == 0:
            part = pbuf[h, x, 1 - zl].astype(F32)
            for d in range(3):
                part += rbuf[h, 2 * d + 1 - zl].astype(F32)
            pbuf[h, x, 1 - zl] = part.astype(BF16)
        else:
            for d in range(1, 4):
                pbuf[h, xm(d), zl] = (pbuf[h, xm(d), zl].astype(F32) + rbuf[h, xm(d)].astype(F32)).astype(BF16)
        for copy in second_copies(kind, h):
            copy.start()

    def up_result(h):
        kind = kinds[h]
        for copy in second_copies(kind, h) if kind < 2 else first_copies(kind, h):
            copy.wait_recv()
        out = pbuf[h, x, zl].astype(F32)
        if kind == 0:
            pieces = [2 * d + zl for d in range(3)] + [6]
        elif kind == 1:
            pieces = [x, 4, 5, 6]
        else:
            pieces = list(range(7))
        for piece in pieces:
            out += rbuf[h, piece].astype(F32)
        return out

    def head_tile(h, t):
        rows = pl.ds(pl.multiple_of(t * TILE, TILE), TILE)
        hcols = pl.ds(pl.multiple_of(h * HD, HD), HD)
        kcols = pl.ds(pl.multiple_of(h * 256, 256), 256)
        prob = ebuf[h, rows, :] * wst[h, pl.ds(t, 1), :]
        gs = (prob * (gbuf[h, rows, :] - delta[pl.ds(h, 1), :]) * SCALE).astype(BF16)
        acc[...] += lax.dot_general(gs, kk[rows, kcols], TN, preferred_element_type=F32)
        gk = dot(gs, q_ref[:, hcols]).astype(BF16)
        gv = dot(prob.astype(BF16), go_ref[:, hcols]).astype(BF16)
        kk[rows, kcols] = jnp.concatenate([gk, gv], axis=1)

    def head_sums(h):
        kcols = pl.ds(pl.multiple_of(h * 256, 256), 256)
        gq = acc[:, 0:HD] + acc[:, HD:2 * HD]
        up = dot(lat_t[...], kk[:, kcols]).astype(BF16)
        for c in range(8):
            pbuf[h, c // 2, c % 2, 0:64, :] = up[c * 64:c * 64 + 64, :]
            pbuf[h, c // 2, c % 2, 64:80, :] = jnp.concatenate(
                [gq[c * 32:c * 32 + 16], gq[c * 32 + 16:c * 32 + 32]], axis=1
            ).astype(BF16)

    def launch(kind, h):
        for copy in first_copies(kind, h):
            copy.start()

    @pl.loop(0, NH - 1)
    def _(h):
        acc[...] = jnp.zeros_like(acc)
        for t in range(8):
            head_tile(h, t)
        head_sums(h)

        @pl.when(jnp.logical_and(h < 6, h % 2 == 0))
        def _():
            launch(0, h)

        @pl.when(jnp.logical_and(h < 6, h % 2 == 1))
        def _():
            launch(1, h)

        @pl.when(h == 5)
        def _():
            pass_on(0)

        @pl.when(h == 6)
        def _():
            launch(2, h)
            pass_on(1)

    sends = ((1, 1), (1, 3), (1, 2), (1, 0), (0, 2), (0, 1), (0, 3), (0, 0))

    def pairwise(i):
        return remote(gds.at[i], gdr.at[i], gd_send.at[i], gd_recv.at[i], partner)

    def tile_of(i):
        z_, d = sends[i]
        return (zh if z_ == 0 else oz) * 4 + ym(d)

    def latent_tile(i):
        t = tile_of(i)
        part = dot(kk[pl.ds(pl.multiple_of(t * TILE, TILE), TILE), :], up_t[...])
        for b in range(2):
            cols = slice(b * 256, (b + 1) * 256)
            ebuf[i, b * 256:(b + 1) * 256, :] = part[:, cols]
            gds[i, :, cols] = ebuf[i, pl.ds(pl.multiple_of(b * 256 + (1 - core) * 128, 128), 128), :].astype(BF16)
        pairwise(i).start()

    def held(i, b):
        rows = pl.ds(pl.multiple_of(b * 256 + core * 128, 128), 128)
        return ebuf[i, rows, :] + gdr[i, :, b * 256:(b + 1) * 256].astype(F32)

    def lat_copy(i):
        return remote(ls.at[i], lr.at[i], l_send.at[i], l_recv.at[i], chip(*sends[i]))

    def lat_send(i):
        pairwise(i).wait_recv()
        for b in range(2):
            ls[i, :, b * 256:(b + 1) * 256] = held(i, b).astype(BF16)
        lat_copy(i).start()

    acc[...] = jnp.zeros_like(acc)
    head_tile(NH - 1, tile_of(0))
    latent_tile(0)
    for i in range(1, 8):
        head_tile(NH - 1, tile_of(i))
    for i in range(1, 8):
        latent_tile(i)
        if i == 1:
            lat_send(0)
        if i >= 3:
            lat_send(i - 2)
        if i == 3:
            head_sums(NH - 1)
            launch(2, NH - 1)
        if i % 2 == 1:
            pass_on(2 + i // 2)
    lat_send(6)
    for h in range(NH):
        out = up_result(h)
        cols = slice(h * HD, (h + 1) * HD)
        gk_out[:, cols] = out[0:64, 0:HD]
        gv_out[:, cols] = out[0:64, HD:2 * HD]
        gq_out[0:16, cols] = out[64:80, 0:HD]
        gq_out[16:32, cols] = out[64:80, HD:2 * HD]
    leaving = [
        pltpu.make_async_copy(src, dst, out_sem.at[i])
        for i, (src, dst) in enumerate(((gq_out, gq_hbm), (gk_out, gk_hbm), (gv_out, gv_hbm), (gl_out, gl_hbm)))
    ]
    for copy in leaving[:3]:
        copy.start()
    pairwise(7).wait_recv()
    for i in range(7):
        lat_copy(i).wait_recv()
    for b in range(2):
        out = held(7, b)
        for i in range(7):
            out += lr[i, :, b * 256:(b + 1) * 256].astype(F32)
        gl_out[:, b * 256:(b + 1) * 256] = out

    leaving[3].start()

    for copy in leaving:
        copy.wait()
    ag(0, own_slot, partner).wait_send()
    for k in range(1, 8):
        outgoing(k).wait_send()
        forward(k).wait_send()
    for d in range(1, 8):
        stat(0, d, ci).wait_send()
    for h in range(NH):
        for copy in first_copies(kinds[h], h) + second_copies(kinds[h], h):
            copy.wait_send()
    for i in range(8):
        pairwise(i).wait_send()
    for i in range(7):
        lat_copy(i).wait_send()


def settle(*refs):
    sources, results, buffers = refs[:4], refs[4:8], refs[8:12]
    in_sem, out_sem = refs[12:]
    loads = [pltpu.make_async_copy(sources[i], buffers[i], in_sem.at[i]) for i in range(4)]
    stores = [pltpu.make_async_copy(buffers[i], results[i], out_sem.at[i]) for i in range(4)]
    for load in loads:
        load.start()
    for load, store in zip(loads, stores):
        load.wait()
        store.start()
    for store in stores:
        store.wait()


def local(queries, grad_out, latent, up_key, up_value):
    dma = pltpu.SemaphoreType.DMA
    vmem = pltpu.VMEM
    place = pl.BlockSpec(memory_space=pl.ANY)
    shape = jax.ShapeDtypeStruct
    results = (
        shape((32, 1024), F32), shape((128, 512), F32),
        shape((64, 1024), F32), shape((64, 1024), F32),
    )
    sums = pl.pallas_call(
        kernel,
        out_shape=results,
        in_specs=[place] * 5,
        out_specs=(place,) * 4,
        scratch_shapes=[
            *(vmem(r.shape, F32) for r in results), dma((4,)),
            vmem((NQ, 1024), BF16), vmem((NQ, 1024), BF16), vmem((512, 1024), BF16), vmem((512, 1024), BF16),
            vmem((ROWS, 512), BF16), vmem((512, ROWS), BF16), vmem((2048, 512), BF16),
            vmem((NH, HD, NQ), BF16), vmem((NH, HD, NQ), BF16),
            vmem((ROWS, 2048), BF16), vmem((NH, ROWS, NQ), F32), vmem((NH, ROWS, NQ), F32),
            vmem((TILE, NQ), F32),
            vmem((NH, 8, NQ), F32), vmem((NH, 8, NQ), F32), vmem((NH, 8, NQ), F32),
            vmem((1, 8, 3 * NH, NQ), F32), vmem((NH, 8, NQ), F32), vmem((NH, NQ), F32),
            vmem((256, 256), F32),
            vmem((NH, 4, 2, 80, 256), BF16), vmem((NH, 7, 80, 256), BF16),
            vmem((8, 128, 512), BF16), vmem((8, 128, 512), BF16), vmem((7, 128, 512), BF16), vmem((7, 128, 512), BF16),
            dma((5,)), dma((15,)), dma((16,)), dma((1, 7)), dma((1, 8)), dma((NH, 7)), dma((NH, 7)),
            dma((8,)), dma((8,)), dma((7,)), dma((7,)),
        ],
        compiler_params=pltpu.CompilerParams(
            collective_id=0, has_side_effects=True, vmem_limit_bytes=67043328
        ),
    )(queries, grad_out, latent, up_key, up_value)
    return pl.pallas_call(
        settle,
        out_shape=results,
        in_specs=[place] * 4,
        out_specs=(place,) * 4,
        scratch_shapes=[*(vmem(r.shape, F32) for r in results), dma((4,)), dma((4,))],
    )(*sums)


def solution(mesh):
    return jax.shard_map(
        local,
        mesh=mesh,
        in_specs=(
            P(None, "head"),
            P(None, "head"),
            P(("ctx", "head"), None),
            P(None, "head"),
            P(None, "head"),
        ),
        out_specs=(P("ctx", "head"), P(("ctx", "head"), None), P("ctx", "head"), P("ctx", "head")),
        check_vma=False,
    )
```
